256 devices in a mesh: site: 32 (over z, x), real: 8 (over y, core).
Axes of the slice: x: 4, y: 4, z: 8, core: 2. Of those that a mesh axis runs over, the one named last changes fastest.
Arguments:
- epsilon: bfloat16 [32768, 4096], P('site', 'real'), may hold values from -6 to 6
- factor: bfloat16 [2, 288, 512, 512], P(None, 'site'), may hold values from -0.09375 to 0.09375
- block_rows: int32 [2, 288], P(None, 'site'), may hold values from 0 to 63, as said below
- median_log: float32 [32768], P('site'), may hold values from -2.5 to -0.5
- spread_log: float32 [32768], P('site'), may hold values from 0.4 to 0.8
- critical_yield: float32 [32768], P('site'), may hold values from 0.03 to 0.3
Outputs:
- residual_field: bfloat16 [32768, 4096], P('site', 'real')
- mean_damage: float32 [32768], P('site')
The draws below stay inside these ranges and needn't reach their ends.
Inputs may be any that keep to these rules, and one draw needn't show every extreme that they name: block_rows[p, b] = (c + o) mod 64, with c = 2 * (b // 9) + p the block's column tile and o in 0 to 11; the offsets o of one block column are distinct, and the first block of each column has o = 0.
All inputs are finite; a program needn't handle non-finite values.
Results may differ from the reference program's by a relative error of at most 0.001.
Values sent between devices are 32-bit elements; how exact they have to be, the bound alone decides.
No kernel may reach another device: no remote copies, remote signals or barrier semaphores. Data moves between devices by JAX's collectives and lax.ppermute only.
A program may use at most 256 MiB of HBM per device.

```python
import math
import jax
import jax.numpy as jnp
from jax import lax

TILE = 512
PANELS = 2
BLOCKS = 9
BAND = 12
TILES = 64
NBLK = 288
SITES = 32768
REALS = 4096


def draw_block_rows(key, part):
    columns = TILES // PANELS
    scores = jax.random.randint(key, (PANELS, columns, BAND - 1), 0, 1 << 20) * BAND
    scores = scores + jnp.arange(BAND - 1, dtype=jnp.int32)
    chosen = jnp.argsort(scores, axis=-1)[:, :, :BLOCKS - 1].astype(jnp.int32) + 1
    offsets = jnp.concatenate([jnp.zeros((PANELS, columns, 1), jnp.int32), chosen], axis=-1)
    column_tile = PANELS * jnp.arange(columns, dtype=jnp.int32)[None, :, None] + jnp.arange(PANELS, dtype=jnp.int32)[:, None, None]
    result = (column_tile + offsets) % TILES
    return result.reshape(PANELS, columns * BLOCKS).astype(jnp.int32)


def levels(rng, shape, pieces, least, high):
    level = 1.0
    for position, blocks in pieces:
        steps = jax.random.uniform(jax.random.fold_in(jax.random.fold_in(rng, 6), position), (blocks,), jnp.float32, least / len(pieces), high / len(pieces))
        level = level * jnp.repeat(jnp.exp(steps), shape[position] // blocks).reshape((-1,) + (1,) * (len(shape) - 1 - position))
    return level


def centred(own_key, extent, spread, most, cuts=(), kind=jnp.bfloat16):
    gain = levels(own_key, extent, cuts, -0.22, 0.18) if cuts else 1.0
    drawn = jax.random.normal(own_key, extent, jnp.float32) * spread * gain
    return jnp.minimum(jnp.maximum(drawn, -most), most).astype(kind)


def setup_inputs(seed: int = 0) -> dict:
    streams_of = jax.random.split(jax.random.key(seed), 7)
    return {
        "epsilon": centred(streams_of[0], (SITES, REALS), 1.0, 6.0, ((0, 32), (1, 8))),
        "factor": centred(streams_of[1], (PANELS, NBLK, TILE, TILE), (TILE * BLOCKS) ** -0.5, 0.09375, ((1, 32),)),
        "block_rows": draw_block_rows(jax.random.fold_in(streams_of[6], 71), 0),
        "median_log": jnp.clip(-2.5 + 2.0 * jax.random.uniform(streams_of[3], (SITES,), jnp.float32) ** levels(streams_of[3], (SITES,), ((0, 32),), -0.2, 0.2), -2.5, -0.5),
        "spread_log": jnp.clip(0.4 + 0.4 * jax.random.uniform(streams_of[4], (SITES,), jnp.float32) ** levels(streams_of[4], (SITES,), ((0, 32),), -0.2, 0.2), 0.4, 0.8),
        "critical_yield": jnp.clip(jnp.exp(math.log(0.3) - 2.3025852 * jax.random.uniform(streams_of[5], (SITES,), jnp.float32) ** levels(streams_of[5], (SITES,), ((0, 32),), -0.2, 0.2)), 0.03, 0.3),
    }


coeff_disp = 10.0 ** 0.215
power_margin = 2.341
power_ratio = 1.438


def reference(epsilon, factor, block_rows, median_log, spread_log, critical_yield):
    tiles = SITES // TILE
    draws = epsilon.reshape(tiles, TILE, REALS)
    field = jnp.zeros((tiles, TILE, REALS), jnp.float32)
    for panel in range(PANELS):
        def add_block(carry, item):
            block, target, number = item
            column = (PANELS * (number // BLOCKS) + panel).astype(jnp.int32)
            source = lax.dynamic_index_in_dim(draws, column, 0, keepdims=False)
            product = jnp.dot(block, source, preferred_element_type=jnp.float32)
            return carry.at[target].add(product), None
        numbers = jnp.arange(NBLK, dtype=jnp.int32)
        field, unused = lax.scan(add_block, field, (factor[panel], block_rows[panel], numbers))
    residual_field = field.astype(jnp.bfloat16).reshape(SITES, REALS)
    log_peak = median_log[:, None] + spread_log[:, None] * residual_field.astype(jnp.float32)
    log_ratio = jnp.log(critical_yield)[:, None] - log_peak
    ratio = jnp.exp(log_ratio)
    margin = jnp.maximum(1.0 - ratio, 0.0)
    displacement = coeff_disp * jnp.power(margin, power_margin) * jnp.exp(-power_ratio * log_ratio)
    mean_damage = jnp.sum(jnp.log1p(displacement), axis=1) / REALS
    return residual_field, mean_damage
```

```python
import jax
import jax.numpy as jnp
from jax import lax
from jax.experimental import pallas as pl
from jax.experimental.pallas import tpu as pltpu
from jax.sharding import PartitionSpec as P

COLUMNS = 4
CHUNKS = ((1, 0, 192), (1, 192, 512), (0, 0, 320), (0, 320, 512))
NONE = 13

coeff_disp = 10.0**0.215
power_margin = 2.341
power_ratio = 1.438

UP = {c: (1, c) for c in range(4)}
RIGHT = {0: (0, 1), 1: (0, 2), 2: (0, 3), 3: (0, 0)}
LEFT = {0: (0, 3), 1: (0, 0), 2: (0, 1), 3: (0, 2)}
CROSS = {0: (0, 2), 1: (0, 3), 2: (0, 0), 3: (0, 1)}
DOWN = {c: (-1, c) for c in range(4)}
MOSTLY_DOWN = {0: (-1, 0), 1: (-1, 1), 2: (-1, 2), 3: (1, 3)}
HALF_DOWN = {0: (-1, 0), 1: (-1, 1), 2: (1, 2), 3: (1, 3)}
TWICE_UP = {0: (2, 0)}


def slot_sums(plan):
    def body(rows_ref, factor_ref, draws_ref, *refs):
        outs = refs[: sum(len(cuts) for _, cuts in plan)]
        table, blocks_ref, sums_ref, draws_vmem, in_sem, draws_sem, out_sem = refs[len(outs) :]
        panels, blocks = factor_ref.shape[:2]
        site = lax.axis_index("site")
        tiles = panels * lax.axis_size("site")
        column = lax.rem(site, COLUMNS)
        load = pltpu.make_async_copy(draws_ref, draws_vmem, draws_sem)
        load.start()
        for p in range(panels):
            for slot in range(NONE + 1):
                table[p, slot] = -1
        for p in range(panels):
            for b in range(blocks):
                table[p, lax.rem(rows_ref[p, b] - panels * site + tiles, tiles)] = b
        found, loads = [], []
        for i, (slot_of, _) in enumerate(plan):
            slot = slot_of(column)
            for p in range(panels):
                b = table[p, slot]
                found.append(b)
                copy = pltpu.make_async_copy(
                    factor_ref.at[p, jnp.maximum(b, 0)], blocks_ref.at[panels * i + p], in_sem.at[panels * i + p]
                )
                copy.start()
                loads.append(copy)
        load.wait()
        stores = []
        for i, (_, cuts) in enumerate(plan):
            for p in range(panels):
                n = panels * i + p
                loads[n].wait()
                b = found[n]

                @pl.when(b >= 0)
                def _():
                    product = jnp.dot(blocks_ref[n], draws_vmem[p], preferred_element_type=jnp.float32)
                    if p == 0:
                        sums_ref[i] = product
                    else:
                        sums_ref[i] += product

                if p == 0:

                    @pl.when(b < 0)
                    def _():
                        sums_ref[i] = jnp.zeros(sums_ref.shape[1:], jnp.float32)

            for low, high in cuts:
                k = len(stores)
                copy = pltpu.make_async_copy(sums_ref.at[i, pl.ds(low, high - low)], outs[k], out_sem.at[k])
                copy.start()
                stores.append(copy)
        for copy in stores:
            copy.wait()

    return body


def sums_of(plan, block_rows, factor, draws):
    panels, blocks, tile, _ = factor.shape
    reals = draws.shape[-1]
    count = len(plan)
    sizes = [high - low for _, cuts in plan for low, high in cuts]
    anywhere = pl.BlockSpec(memory_space=pl.ANY)
    return pl.pallas_call(
        slot_sums(plan),
        in_specs=[pl.BlockSpec(memory_space=pltpu.SMEM), anywhere, anywhere],
        out_specs=[anywhere] * len(sizes),
        out_shape=[jax.ShapeDtypeStruct((n, reals), jnp.float32) for n in sizes],
        scratch_shapes=[
            pltpu.SMEM((2, 16), jnp.int32),
            pltpu.VMEM((panels * count, tile, tile), factor.dtype),
            pltpu.VMEM((count, tile, reals), jnp.float32),
            pltpu.VMEM(draws.shape, draws.dtype),
            pltpu.SemaphoreType.DMA((panels * count,)),
            pltpu.SemaphoreType.DMA,
            pltpu.SemaphoreType.DMA((len(sizes),)),
        ],
        cost_estimate=pl.CostEstimate(
            flops=2 * panels * count * tile * tile * reals,
            bytes_accessed=panels * count * tile * tile * 2 + count * tile * reals * 4,
            transcendentals=0,
        ),
        compiler_params=pltpu.CompilerParams(vmem_limit_bytes=56 << 20),
    )(block_rows, factor, draws)


def after(value, *others):
    return lax.optimization_barrier((value, *others))[0]


def shards(epsilon, factor, block_rows, median_log, spread_log, critical_yield):
    panels = factor.shape[0]
    tile_size = factor.shape[-1]
    own_reals = epsilon.shape[1]
    planes = lax.axis_size("site") // COLUMNS
    column = lax.rem(lax.axis_index("site"), COLUMNS)
    draws = epsilon.reshape(panels, tile_size, own_reals)

    def send(value, moves):
        pairs = []
        for z in range(planes):
            for x, (up, target) in moves.items():
                pairs.append((z * COLUMNS + x, ((z + up) % planes) * COLUMNS + target))
        return lax.ppermute(value, "site", pairs)

    def at(slot):
        return lambda c: slot

    whole = ((0, tile_size),)
    cuts = [tuple((low, high) for t, low, high in CHUNKS if t == tile) for tile in range(panels)]
    first = [
        (at(3), cuts[1]),
        (at(5), whole),
        (lambda c: jnp.where(c < 2, 4, 12), whole),
        (at(7), whole),
    ]
    rest = [
        (at(11), whole),
        (lambda c: jnp.where(c < 3, 2, 10), cuts[0]),
        (lambda c: jnp.where(c < 2, 12, 4), whole),
        (at(6), whole),
        (at(9), whole),
        (lambda c: jnp.where(c < 3, 10, 2), whole),
        (at(8), whole),
        (at(1), whole),
        (at(0), whole),
    ]
    *away1, second1, second0, third1 = sums_of(first, block_rows, factor, draws)
    far1, *away0, kept0, third0, fourth1, far0, fourth0, own1, own0 = sums_of(rest, block_rows, factor, draws)
    aways = {1: away1, 0: away0}
    fars, fourths, owns = {1: far1, 0: far0}, {1: fourth1, 0: fourth0}, {1: own1, 0: own0}

    near = [None] * len(CHUNKS)
    near[0] = send(away1[0], DOWN)
    crossed1 = send(second1, CROSS)
    left1 = send(third1, LEFT)
    vertical = send(second0, HALF_DOWN)
    crossed0 = send(kept0 + vertical, CROSS)
    left0 = send(after(third0, left1), LEFT)
    crossed, lefts = {1: crossed1, 0: crossed0}, {1: left1, 0: left0}

    log_yield = jnp.log(critical_yield)
    fields, totals = {}, {}
    for n, (t, low, high) in enumerate(CHUNKS):
        rows = slice(low, high)
        if n:
            away = aways[t][[c[:2] for c in CHUNKS if c[0] == t].index((t, low))]
            near[n] = send(after(away, crossed1, near[n - 1]), DOWN if t else MOSTLY_DOWN)
        right = send(fars[t][rows] + near[n], RIGHT)
        left, cross = lefts[t][rows], crossed[t][rows]
        onward = fourths[t][rows] + jnp.where(column == 3, 0.0, left)
        field = owns[t][rows] + jnp.where(column == 3, left, 0.0)
        if t:
            onward = onward + jnp.where(column == 0, 0.0, right) + jnp.where(column < 2, cross, 0.0)
            field = field + jnp.where(column < 2, 0.0, cross) + send(right, TWICE_UP)
        else:
            onward = onward + right + cross
        field = (field + send(onward, UP)).astype(jnp.bfloat16)
        here = slice(t * tile_size + low, t * tile_size + high)
        log_peak = median_log[here, None] + spread_log[here, None] * field.astype(jnp.float32)
        log_ratio = log_yield[here, None] - log_peak
        ratio = jnp.exp(log_ratio)
        margin = jnp.maximum(1.0 - ratio, 0.0)
        displacement = coeff_disp * jnp.power(margin, power_margin) * jnp.exp(-power_ratio * log_ratio)
        fields[t, low] = field
        totals[t, low] = jnp.sum(jnp.log1p(displacement), axis=1)
    order = sorted(fields)
    residual_field = jnp.concatenate([fields[k] for k in order], axis=0)
    local_total = jnp.concatenate([totals[k] for k in order], axis=0)
    reals = lax.axis_size("real")
    copies = jnp.broadcast_to(local_total[None], (reals, local_total.shape[0]))
    everything = lax.all_to_all(copies, "real", 0, 0, tiled=True)
    mean_damage = jnp.sum(everything, axis=0) / (own_reals * reals)
    return residual_field, mean_damage


def solution(mesh):
    return jax.shard_map(
        shards,
        mesh=mesh,
        in_specs=(
            P("site", "real"),
            P(None, "site", None, None),
            P(None, "site"),
            P("site"),
            P("site"),
            P("site"),
        ),
        out_specs=(P("site", "real"), P("site")),
        check_vma=False,
    )
```

```python
import jax
import jax.numpy as jnp
from jax import lax
from jax.experimental import pallas as pl
from jax.experimental.pallas import tpu as pltpu
from jax.sharding import PartitionSpec as P

COLUMNS = 4
PIECES = ((0, 256), (256, 512))
NONE = 13

coeff_disp = 10.0**0.215
power_margin = 2.341
power_ratio = 1.438

UP = {c: (1, c) for c in range(4)}
RIGHT = {0: (0, 1), 1: (0, 2), 2: (0, 3), 3: (0, 0)}
LEFT = {0: (0, 3), 1: (0, 0), 2: (0, 1), 3: (0, 2)}
CROSS = {0: (0, 2), 1: (0, 3), 2: (0, 0), 3: (0, 1)}
MOSTLY_DOWN = {0: (-1, 0), 1: (-1, 1), 2: (-1, 2), 3: (1, 3)}
HALF_DOWN = {0: (-1, 0), 1: (-1, 1), 2: (1, 2), 3: (1, 3)}


def slot_sums(plan):
    def body(rows_ref, factor_ref, draws_ref, *refs):
        outs = refs[: sum(len(cuts) for _, cuts in plan)]
        table, blocks_ref, sums_ref, draws_vmem, in_sem, draws_sem, out_sem = refs[len(outs) :]
        panels, blocks, side = factor_ref.shape[:3]
        site = lax.axis_index("site")
        tiles = panels * lax.axis_size("site")
        column = lax.rem(site, COLUMNS)
        load = pltpu.make_async_copy(draws_ref, draws_vmem, draws_sem)
        load.start()
        for p in range(panels):
            for slot in range(NONE + 1):
                table[p, slot] = -1
        for p in range(panels):
            for b in range(blocks):
                table[p, lax.rem(rows_ref[p, b] - panels * site + tiles, tiles)] = b
        found, loads = [], []
        for i, (slot_of, _) in enumerate(plan):
            slot = slot_of(column)
            for p in range(panels):
                b = table[p, slot]
                found.append(b)
                copy = pltpu.make_async_copy(
                    factor_ref.at[p, jnp.maximum(b, 0)],
                    blocks_ref.at[i, :, pl.ds(p * side, side)],
                    in_sem.at[panels * i + p],
                )
                copy.start()
                loads.append(copy)
        load.wait()
        stores = []
        for i, (_, cuts) in enumerate(plan):
            for p in range(panels):
                n = panels * i + p
                loads[n].wait()

                @pl.when(found[n] < 0)
                def _():
                    blocks_ref[i, :, pl.ds(p * side, side)] = jnp.zeros((side, side), blocks_ref.dtype)

            sums_ref[i] = jnp.dot(blocks_ref[i], draws_vmem[...], preferred_element_type=jnp.float32)
            for low, high in cuts:
                k = len(stores)
                copy = pltpu.make_async_copy(sums_ref.at[i, pl.ds(low, high - low)], outs[k], out_sem.at[k])
                copy.start()
                stores.append(copy)
        for copy in stores:
            copy.wait()

    return body


def sums_of(plan, block_rows, factor, draws, cost):
    panels, blocks, tile, _ = factor.shape
    reals = draws.shape[-1]
    count = len(plan)
    sizes = [high - low for _, cuts in plan for low, high in cuts]
    anywhere = pl.BlockSpec(memory_space=pl.ANY)
    return pl.pallas_call(
        slot_sums(plan),
        in_specs=[pl.BlockSpec(memory_space=pltpu.SMEM), anywhere, anywhere],
        out_specs=[anywhere] * len(sizes),
        out_shape=[jax.ShapeDtypeStruct((n, reals), jnp.float32) for n in sizes],
        scratch_shapes=[
            pltpu.SMEM((2, 16), jnp.int32),
            pltpu.VMEM((count, tile, panels * tile), factor.dtype),
            pltpu.VMEM((count, tile, reals), jnp.float32),
            pltpu.VMEM(draws.shape, draws.dtype),
            pltpu.SemaphoreType.DMA((panels * count,)),
            pltpu.SemaphoreType.DMA,
            pltpu.SemaphoreType.DMA((len(sizes),)),
        ],
        cost_estimate=pl.CostEstimate(flops=cost, bytes_accessed=cost, transcendentals=0),
        compiler_params=pltpu.CompilerParams(vmem_limit_bytes=56 << 20),
    )(block_rows, factor, draws)


def after(value, *others):
    return lax.optimization_barrier((value, *others))[0]


def shards(epsilon, factor, block_rows, median_log, spread_log, critical_yield):
    panels = factor.shape[0]
    tile_size = factor.shape[-1]
    own_reals = epsilon.shape[1]
    planes = lax.axis_size("site") // COLUMNS
    column = lax.rem(lax.axis_index("site"), COLUMNS)

    def send(value, moves):
        pairs = []
        for z in range(planes):
            for x, (up, target) in moves.items():
                pairs.append((z * COLUMNS + x, ((z + up) % planes) * COLUMNS + target))
        return lax.ppermute(value, "site", pairs)

    def at(slot):
        return lambda c: slot

    whole = ((0, tile_size),)
    first = [(at(5), whole), (lambda c: jnp.where(c < 3, 3, 11), whole)]
    second = [(at(7), whole), (lambda c: jnp.where(c < 2, 4, 12), whole)]
    third = [(lambda c: jnp.where(c < 3, 11, 3), whole), (lambda c: jnp.where(c < 3, 2, 10), whole), (lambda c: jnp.where(c < 2, 12, 4), whole)]
    rest = [
        (at(6), PIECES),
        (at(9), whole),
        (lambda c: jnp.where(c < 3, 10, 2), whole),
        (at(8), whole),
        (at(1), whole),
        (at(0), whole),
    ]
    second1, away1 = sums_of(first, block_rows, factor, epsilon, 1 << 20)
    third1, second0 = sums_of(second, after(block_rows, second1), factor, epsilon, 1 << 10)
    far1, away0, kept0 = sums_of(third, after(block_rows, second0), factor, epsilon, 1 << 10)

    last = column == 3
    low = column < 2
    cross1 = send(second1, CROSS)
    near1 = send(away1, MOSTLY_DOWN)
    left1 = send(after(third1, cross1), LEFT)
    vertical = send(second0, HALF_DOWN)
    right1 = send(after(far1, cross1) + near1, RIGHT)
    *third0, fourth1, far0, fourth0, own1, own0 = sums_of(rest, after(block_rows, near1), factor, epsilon, 1 << 10)
    middle0 = after(kept0, own0) + vertical
    cross0 = send(middle0, CROSS)
    near0 = send(after(away0, right1, middle0), MOSTLY_DOWN)
    onward1 = fourth1 + right1 + jnp.where(last, 0.0, left1) + jnp.where(low, cross1, 0.0)
    up1 = send(onward1, UP)
    own1 = own1 + jnp.where(low, 0.0, cross1)
    results = [(1, 0, tile_size, own1, up1, left1)]
    before, ready = left1, onward1
    for (start, end), third in zip(PIECES, third0):
        rows = slice(start, end)
        left0 = send(after(third, before), LEFT)
        right0 = send(far0[rows] + near0[rows], RIGHT)
        onward0 = after(fourth0, ready)[rows] + right0 + cross0[rows] + jnp.where(last, 0.0, left0)
        results.append((0, start, end, own0[rows], send(onward0, UP), left0))
        before, ready = left0, onward0

    log_yield = jnp.log(critical_yield)
    fields, totals = {}, {}
    done = log_yield
    for t, start, end, own, up, left in results:
        field = (after(own, done) + up + jnp.where(last, left, 0.0)).astype(jnp.bfloat16)
        here = slice(t * tile_size + start, t * tile_size + end)
        log_peak = median_log[here, None] + spread_log[here, None] * field.astype(jnp.float32)
        log_ratio = log_yield[here, None] - log_peak
        ratio = jnp.exp(log_ratio)
        margin = jnp.maximum(1.0 - ratio, 0.0)
        displacement = coeff_disp * jnp.power(margin, power_margin) * jnp.exp(-power_ratio * log_ratio)
        fields[t, start] = field
        done = totals[t, start] = jnp.sum(jnp.log1p(displacement), axis=1)
    order = sorted(fields)
    residual_field = jnp.concatenate([fields[k] for k in order], axis=0)
    local_total = jnp.concatenate([totals[k] for k in order], axis=0)
    reals = lax.axis_size("real")
    copies = jnp.broadcast_to(local_total[None], (reals, local_total.shape[0]))
    everything = lax.all_to_all(copies, "real", 0, 0, tiled=True)
    mean_damage = jnp.sum(everything, axis=0) / (own_reals * reals)
    return residual_field, mean_damage


def solution(mesh):
    return jax.shard_map(
        shards,
        mesh=mesh,
        in_specs=(
            P("site", "real"),
            P(None, "site", None, None),
            P(None, "site"),
            P("site"),
            P("site"),
            P("site"),
        ),
        out_specs=(P("site", "real"), P("site")),
        check_vma=False,
    )
```

```python
import jax
import jax.numpy as jnp
from jax import lax
from jax.experimental import pallas as pl
from jax.experimental.pallas import tpu as pltpu
from jax.sharding import PartitionSpec as P

COLUMNS = 4
PIECES = ((0, 256), (256, 512))
NONE = 13

coeff_disp = 10.0**0.215
power_margin = 2.341
power_ratio = 1.438

UP = {c: (1, c) for c in range(4)}
RIGHT = {0: (0, 1), 1: (0, 2), 2: (0, 3), 3: (0, 0)}
LEFT = {0: (0, 3), 1: (0, 0), 2: (0, 1), 3: (0, 2)}
CROSS = {0: (0, 2), 1: (0, 3), 2: (0, 0), 3: (0, 1)}
MOSTLY_DOWN = {0: (-1, 0), 1: (-1, 1), 2: (-1, 2), 3: (1, 3)}
HALF_DOWN = {0: (-1, 0), 1: (-1, 1), 2: (1, 2), 3: (1, 3)}


def slot_sums(plan):
    def body(rows_ref, factor_ref, draws_ref, *refs):
        outs = refs[: sum(len(cuts) for _, cuts in plan)]
        table, blocks_ref, sums_ref, draws_vmem, in_sem, draws_sem, out_sem = refs[len(outs) :]
        panels, blocks, side = factor_ref.shape[:3]
        site = lax.axis_index("site")
        tiles = panels * lax.axis_size("site")
        column = lax.rem(site, COLUMNS)
        load = pltpu.make_async_copy(draws_ref, draws_vmem, draws_sem)
        load.start()
        for p in range(panels):
            for slot in range(NONE + 1):
                table[p, slot] = -1
        for p in range(panels):
            for b in range(blocks):
                table[p, lax.rem(rows_ref[p, b] - panels * site + tiles, tiles)] = b
        found, loads = [], []
        for i, (slot_of, _) in enumerate(plan):
            slot = slot_of(column)
            for p in range(panels):
                b = table[p, slot]
                found.append(b)
                copy = pltpu.make_async_copy(
                    factor_ref.at[p, jnp.maximum(b, 0)],
                    blocks_ref.at[i, :, pl.ds(p * side, side)],
                    in_sem.at[panels * i + p],
                )
                copy.start()
                loads.append(copy)
        load.wait()
        stores = []
        for i, (_, cuts) in enumerate(plan):
            for p in range(panels):
                n = panels * i + p
                loads[n].wait()

                @pl.when(found[n] < 0)
                def _():
                    blocks_ref[i, :, pl.ds(p * side, side)] = jnp.zeros((side, side), blocks_ref.dtype)

            sums_ref[i] = jnp.dot(blocks_ref[i], draws_vmem[...], preferred_element_type=jnp.float32)
            for low, high in cuts:
                k = len(stores)
                copy = pltpu.make_async_copy(sums_ref.at[i, pl.ds(low, high - low)], outs[k], out_sem.at[k])
                copy.start()
                stores.append(copy)
        for copy in stores:
            copy.wait()

    return body


def sums_of(plan, block_rows, factor, draws, cost):
    panels, blocks, tile, _ = factor.shape
    reals = draws.shape[-1]
    count = len(plan)
    sizes = [high - low for _, cuts in plan for low, high in cuts]
    anywhere = pl.BlockSpec(memory_space=pl.ANY)
    return pl.pallas_call(
        slot_sums(plan),
        in_specs=[pl.BlockSpec(memory_space=pltpu.SMEM), anywhere, anywhere],
        out_specs=[anywhere] * len(sizes),
        out_shape=[jax.ShapeDtypeStruct((n, reals), jnp.float32) for n in sizes],
        scratch_shapes=[
            pltpu.SMEM((2, 16), jnp.int32),
            pltpu.VMEM((count, tile, panels * tile), factor.dtype),
            pltpu.VMEM((count, tile, reals), jnp.float32),
            pltpu.VMEM(draws.shape, draws.dtype),
            pltpu.SemaphoreType.DMA((panels * count,)),
            pltpu.SemaphoreType.DMA,
            pltpu.SemaphoreType.DMA((len(sizes),)),
        ],
        cost_estimate=pl.CostEstimate(flops=cost, bytes_accessed=cost, transcendentals=0),
        compiler_params=pltpu.CompilerParams(vmem_limit_bytes=56 << 20),
    )(block_rows, factor, draws)


def after(value, *others):
    return lax.optimization_barrier((value, *others))[0]


def shards(epsilon, factor, block_rows, median_log, spread_log, critical_yield):
    panels = factor.shape[0]
    tile_size = factor.shape[-1]
    own_reals = epsilon.shape[1]
    planes = lax.axis_size("site") // COLUMNS
    column = lax.rem(lax.axis_index("site"), COLUMNS)

    def send(value, moves):
        pairs = []
        for z in range(planes):
            for x, (up, target) in moves.items():
                pairs.append((z * COLUMNS + x, ((z + up) % planes) * COLUMNS + target))
        return lax.ppermute(value, "site", pairs)

    def at(slot):
        return lambda c: slot

    whole = ((0, tile_size),)
    first = [(at(5), whole), (lambda c: jnp.where(c < 3, 3, 11), whole)]
    second = [(at(7), whole), (lambda c: jnp.where(c < 2, 4, 12), whole)]
    third = [(lambda c: jnp.where(c < 3, 11, 3), whole), (lambda c: jnp.where(c < 3, 2, 10), whole), (lambda c: jnp.where(c < 2, 12, 4), whole)]
    rest = [
        (at(6), PIECES),
        (at(9), whole),
        (lambda c: jnp.where(c < 3, 10, 2), whole),
        (at(8), whole),
        (at(1), whole),
        (at(0), whole),
    ]
    second1, away1 = sums_of(first, block_rows, factor, epsilon, 1 << 20)
    third1, second0 = sums_of(second, after(block_rows, second1), factor, epsilon, 1 << 10)
    far1, away0, kept0 = sums_of(third, after(block_rows, second0), factor, epsilon, 1 << 10)

    last = column == 3
    low = column < 2
    cross1 = send(second1, CROSS)
    near1 = send(away1, MOSTLY_DOWN)
    left1 = send(after(third1, cross1), LEFT)
    vertical = send(second0, HALF_DOWN)
    right1 = send(after(far1, cross1) + near1, RIGHT)
    *third0, fourth1, far0, fourth0, own1, own0 = sums_of(rest, after(block_rows, near1), factor, epsilon, 1 << 10)
    middle0 = after(kept0, own0) + vertical
    cross0 = send(middle0, CROSS)
    near0 = send(after(away0, right1, middle0), MOSTLY_DOWN)
    onward1 = fourth1 + right1 + jnp.where(last, 0.0, left1) + jnp.where(low, cross1, 0.0)
    up1 = send(onward1, UP)
    own1 = own1 + jnp.where(low, 0.0, cross1)
    results = [(1, 0, tile_size, own1, up1, left1)]
    before, ready = (left1,), onward1
    for (start, end), third in zip(PIECES, third0):
        rows = slice(start, end)
        left0 = send(after(third, *before), LEFT)
        right0 = send(far0[rows] + near0[rows], RIGHT)
        onward0 = after(fourth0, ready)[rows] + right0 + cross0[rows] + jnp.where(last, 0.0, left0)
        results.append((0, start, end, own0[rows], send(onward0, UP), left0))
        before, ready = (left0, right0), onward0

    log_yield = jnp.log(critical_yield)
    fields, totals = {}, {}
    done = log_yield
    for t, start, end, own, up, left in results:
        field = (after(own, done) + up + jnp.where(last, left, 0.0)).astype(jnp.bfloat16)
        here = slice(t * tile_size + start, t * tile_size + end)
        log_peak = median_log[here, None] + spread_log[here, None] * field.astype(jnp.float32)
        log_ratio = log_yield[here, None] - log_peak
        ratio = jnp.exp(log_ratio)
        margin = jnp.maximum(1.0 - ratio, 0.0)
        displacement = coeff_disp * jnp.power(margin, power_margin) * jnp.exp(-power_ratio * log_ratio)
        fields[t, start] = field
        done = totals[t, start] = jnp.sum(jnp.log1p(displacement), axis=1)
    order = sorted(fields)
    residual_field = jnp.concatenate([fields[k] for k in order], axis=0)
    local_total = jnp.concatenate([totals[k] for k in order], axis=0)
    reals = lax.axis_size("real")
    pair = local_total + lax.ppermute(local_total, "real", [(i, i ^ 1) for i in range(reals)])
    around = [lax.ppermute(pair, "real", [(i, (i + 2 * k) % reals) for i in range(reals)]) for k in (1, 2, 3)]
    everything = (pair + around[1]) + (around[0] + around[2])
    mean_damage = everything / (own_reals * reals)
    return residual_field, mean_damage


def solution(mesh):
    return jax.shard_map(
        shards,
        mesh=mesh,
        in_specs=(
            P("site", "real"),
            P(None, "site", None, None),
            P(None, "site"),
            P("site"),
            P("site"),
            P("site"),
        ),
        out_specs=(P("site", "real"), P("site")),
        check_vma=False,
    )
```
